512 devices in a mesh: rows: 128 (over z, y, core), band: 4 (over x).
Axes of the slice: x: 4, y: 8, z: 8, core: 2. Of those that a mesh axis runs over, the one named last changes fastest.
Arguments:
- frames: bfloat16 [2, 512, 512, 96], P(None, 'rows'), may hold values from -6 to 6
- conv_weight: bfloat16 [3, 3, 96, 128], replicated, may hold values from -0.21875 to 0.21875
- proj_weight: bfloat16 [128, 256], replicated, may hold values from -0.5 to 0.5
- band_start: int32 [128], P('rows'), may hold values from -4 to 4, as said below
- band_count: int32 [128], P('rows'), may hold values from 1 to 8, as said below
- pyramid_grad: bfloat16 [128, 2, 4, 512, 960], P('rows', None, 'band'), may hold values from -6 to 6
Outputs:
- pyramid: bfloat16 [128, 2, 4, 512, 960], P('rows', None, 'band')
- source_grad: float32 [256, 256, 256], P('rows', None, 'band')
- target_grad: float32 [256, 256, 256], P('rows', None, 'band')
The draws below stay inside these ranges and needn't reach their ends.
Inputs may be any that keep to these rules, and one draw needn't show every extreme that they name: Row block b's band covers target blocks b + band_start[b] to b + band_start[b] + band_count[b] - 1, all within b - 4 to b + 4. `band_count`: some row block's band has 8 target blocks and some other's has 1.
All inputs are finite; a program needn't handle non-finite values.
Results may differ from the reference program's by a relative error of at most 0.0034.
Values may be sent and summed in bfloat16 or wider, within the bound.
A program may use at most 128 MiB of HBM per device.

```python
import math
import jax
import jax.numpy as jnp
from jax import lax

IN_CHANNELS = 96
MID_CHANNELS = 128
CHANNELS = 256
LEVELS = 4
ROWS_DEV = 2
COLUMNS = 256
BAND_REACH = 4
SLOTS_DEV = 2
FEAT_ROWS = 256
PIXELS = 512
PYRAMID = 960
SLOTS = 8
N_ROWS = 128
N_BAND = 4


def band_tables(key):
    base = jax.random.fold_in(key, 7)
    keys = jax.random.split(base, 6)
    wide = jax.random.randint(keys[0], (N_ROWS,), 0, 4) == 0
    narrow_count = jax.random.randint(keys[1], (N_ROWS,), 1, SLOTS // 2)
    wide_count = jax.random.randint(keys[2], (N_ROWS,), SLOTS // 2 + 1, SLOTS + 1)
    counts = jnp.where(wide, wide_count, narrow_count)
    last = N_ROWS - 1
    before = N_ROWS - 2
    second = jax.random.randint(keys[4], (), 0, N_ROWS - 2)
    places = jnp.arange(N_ROWS, dtype=jnp.int32)
    counts = jnp.where(places == last, SLOTS, counts)
    counts = jnp.where(places == before, N_BAND, counts)
    counts = jnp.where(places == second, 1, counts)
    starts = jax.random.randint(keys[5], (N_ROWS,), -BAND_REACH, BAND_REACH + 2 - counts)
    starts = jnp.where(places == last, -BAND_REACH, starts)
    starts = jnp.where(places == before, 2 - N_BAND, starts)
    starts = jnp.where(places == second, BAND_REACH, starts)
    return (starts.astype(jnp.int32), counts.astype(jnp.int32))


def draw_band_start(key, part):
    return band_tables(key)[0]


def draw_band_count(key, part):
    return band_tables(key)[1]


def block_scale(stream_key, extent, cuts, low, top_value):
    def one(axis_at, shards_of):
        heights = jax.random.uniform(jax.random.fold_in(jax.random.fold_in(stream_key, 6), axis_at), (shards_of,), jnp.float32, low / len(cuts), top_value / len(cuts))
        return jnp.repeat(jnp.exp(heights), extent[axis_at] // shards_of).reshape((-1,) + (1,) * (len(extent) - axis_at - 1))

    factor_of = one(*cuts[0])
    for cut in cuts[1:]:
        factor_of = factor_of * one(*cut)
    return factor_of


def bell_draw(rng, shape, deviation, most, pieces=(), kind=jnp.bfloat16):
    array = deviation * jax.random.normal(rng, shape, jnp.float32)
    if pieces:
        array = array * block_scale(rng, shape, pieces, -0.22, 0.18)
    return jnp.clip(array, -most, most).astype(kind)


def setup_inputs(seed: int = 0) -> dict:
    key_of = jax.random.split(jax.random.key(seed), 7)
    return {
        "frames": bell_draw(key_of[0], (2, 2 * FEAT_ROWS, 2 * COLUMNS, IN_CHANNELS), 1.0, 6.0, ((1, 128),)),
        "conv_weight": bell_draw(key_of[1], (3, 3, IN_CHANNELS, MID_CHANNELS), (9 * IN_CHANNELS) ** -0.5, 0.21875),
        "proj_weight": bell_draw(key_of[2], (MID_CHANNELS, CHANNELS), MID_CHANNELS ** -0.5, 0.5),
        "band_start": draw_band_start(jax.random.fold_in(key_of[6], 71), 0),
        "band_count": draw_band_count(jax.random.fold_in(key_of[6], 71), 0),
        "pyramid_grad": bell_draw(key_of[5], (N_ROWS, SLOTS_DEV, N_BAND, PIXELS, PYRAMID), 1.0, 6.0, ((0, 128), (2, 4))),
    }


def encode(frames, conv_weight, proj_weight):
    convolved = lax.conv_general_dilated(frames, conv_weight, (2, 2), ((1, 0), (1, 0)), dimension_numbers=('NHWC', 'HWIO', 'NHWC'), preferred_element_type=jnp.float32)
    middle = jax.nn.relu(convolved).astype(jnp.bfloat16)
    flattened = jnp.dot(middle.reshape(-1, MID_CHANNELS), proj_weight, preferred_element_type=jnp.float32)
    return flattened.reshape(2, N_ROWS, PIXELS, CHANNELS)

def pool_levels(correlation):
    row_count = correlation.shape[0]
    levels = []
    for level_index in range(LEVELS):
        group_size = 2 ** level_index
        pooled = correlation.reshape(row_count, ROWS_DEV, COLUMNS // group_size, group_size)
        levels.append(lax.optimization_barrier(jnp.mean(pooled, axis=3)).reshape(row_count, PIXELS // group_size))
    return jnp.concatenate(levels, axis=1)

def spread_levels(gradient):
    row_count = gradient.shape[0]
    summed = gradient[:, :PIXELS]
    column_start = PIXELS
    for level_index in range(1, LEVELS):
        group_size = 2 ** level_index
        level_width = PIXELS // group_size
        level_part = gradient[:, column_start:column_start + level_width].reshape(row_count, ROWS_DEV, level_width // ROWS_DEV, 1)
        spread = jnp.broadcast_to(level_part / group_size, (row_count, ROWS_DEV, level_width // ROWS_DEV, group_size))
        summed = summed + spread.reshape(row_count, PIXELS)
        column_start = column_start + level_width
    return summed

def reference(frames, conv_weight, proj_weight, band_start, band_count, pyramid_grad):
    features = encode(frames, conv_weight, proj_weight)
    margin = jnp.zeros((BAND_REACH, PIXELS, CHANNELS), jnp.float32)
    targets = jnp.concatenate([margin, features[1], margin], axis=0)
    factor = 1.0 / math.sqrt(CHANNELS)
    indices = jnp.arange(N_ROWS, dtype=jnp.int32)
    flat_grad = pyramid_grad.reshape(N_ROWS, SLOTS, PIXELS, PYRAMID)

    def one_block(carried, scanned):
        block_index, band_first, count_here, source, gradients = scanned
        pyramids = []
        source_sum = jnp.zeros((PIXELS, CHANNELS), jnp.float32)
        for slot_index in range(SLOTS):
            weight_on = (slot_index < count_here).astype(jnp.float32)
            window_place = (block_index + band_first + slot_index + BAND_REACH).astype(jnp.int32)
            target = lax.dynamic_index_in_dim(targets, window_place, 0, keepdims=False)
            correlation = jnp.dot(source, target.T, precision=lax.Precision.HIGHEST) * factor * weight_on
            pyramids.append(pool_levels(correlation).astype(jnp.bfloat16))
            grad_corr = spread_levels(gradients[slot_index].astype(jnp.float32)) * weight_on
            source_sum = source_sum + jnp.dot(grad_corr, target, precision=lax.Precision.HIGHEST) * factor
            target_part = jnp.dot(grad_corr.T, source, precision=lax.Precision.HIGHEST) * factor
            current = lax.dynamic_index_in_dim(carried, window_place, 0, keepdims=False)
            carried = lax.dynamic_update_index_in_dim(carried, current + target_part, window_place, 0)
        return (carried, (jnp.stack(pyramids), source_sum))
    initial = jnp.zeros((N_ROWS + 2 * BAND_REACH, PIXELS, CHANNELS), jnp.float32)
    carried, outputs = lax.scan(one_block, initial, (indices, band_start, band_count, features[0], flat_grad))
    pyramid, source_grad = outputs
    target_grad = carried[BAND_REACH:BAND_REACH + N_ROWS]
    pyramid = pyramid.reshape(N_ROWS, SLOTS_DEV, N_BAND, PIXELS, PYRAMID)
    return (pyramid, source_grad.reshape(FEAT_ROWS, COLUMNS, CHANNELS), target_grad.reshape(FEAT_ROWS, COLUMNS, CHANNELS))
```

```python
import jax
import jax.numpy as jnp
from jax import lax
from jax.experimental import pallas as pl
from jax.experimental.pallas import tpu as pltpu
from jax.sharding import PartitionSpec as P

ROWS_DEV = 2
BAND_REACH = 4
PIXELS = 512
MID = 128
LOWER = 448
BANDS = 4
QUARTER = PIXELS // BANDS
SHARE = 64
SCALE = 1.0 / 16.0
F32 = jnp.float32
BF16 = jnp.bfloat16


def shifted(x, axis, by):
    size = lax.axis_size(axis)
    pairs = [(i, i + by) for i in range(size) if 0 <= i + by < size]
    return lax.ppermute(x, axis, pairs)


def halves(x):
    high = x.astype(BF16)
    return high, (x - high.astype(F32)).astype(BF16)


def dot(a, b, da=1, db=0):
    return lax.dot_general(a, b, (((da,), (db,)), ((), ())), preferred_element_type=F32)


def tile_kernel(count_ref, source_ref, target_ref, grad_ref, proj_ref, pyramid_ref, terms_ref, share_ref, pool, pair, total):
    j = pl.program_id(0)
    source = source_ref[...]

    @pl.when(j == 0)
    def _():
        row = lax.broadcasted_iota(jnp.int32, (LOWER, PIXELS), 0)
        column = lax.broadcasted_iota(jnp.int32, (LOWER, PIXELS), 1)
        shift = jnp.where(row < 256, 1, jnp.where(row < 384, 2, 3))
        first = jnp.where(row < 256, 0, jnp.where(row < 384, 256, 384))
        weight = jnp.where(row < 256, 0.5, jnp.where(row < 384, 0.25, 0.125))
        pool[...] = jnp.where((column >> shift) == row - first, weight, 0.0).astype(BF16)
        square_high, square_low = halves(dot(proj_ref[...], proj_ref[...], 1, 1) * SCALE)
        high, low = halves(dot(source, square_high) + dot(source, square_low))
        pair[...] = jnp.concatenate([high, low], axis=1)

    valid = j * BANDS + lax.axis_index("band") < count_ref[0]
    target = target_ref[0]
    grad = grad_ref[0, 0, 0]
    high, low = halves(dot(pool[...], target))
    base = dot(pair[...], jnp.concatenate([target, target], axis=1), 1, 1)
    rest = dot(pair[...], jnp.concatenate([high, high], axis=1), 1, 1) + dot(pair[:, :MID], low, 1, 1)
    pyramid_ref[0, 0, 0, :, :PIXELS] = jnp.where(valid, base, 0.0).astype(BF16)
    pyramid_ref[0, 0, 0, :, PIXELS:] = jnp.where(valid, rest, 0.0).astype(BF16)
    both = dot(grad[:, PIXELS:], jnp.concatenate([high, low], axis=1))
    part = jnp.where(valid, dot(grad[:, :PIXELS], target) + both[:, :MID] + both[:, MID:], 0.0)
    spread = dot(source, grad, 0, 0)
    high, low = halves(spread[:, PIXELS:])
    term = (spread[:, :PIXELS] + dot(high, pool[...]) + dot(low, pool[...])) * SCALE
    term = jnp.where(valid, term, 0.0).astype(BF16)
    for q in range(BANDS):
        terms_ref[q, 0] = term[:, q * QUARTER : (q + 1) * QUARTER]

    @pl.when(j == 0)
    def _():
        total[...] = part

    @pl.when(j == 1)
    def _():
        high, low = halves((total[...] + part) * SCALE)
        proj = proj_ref[...]
        wide = dot(proj, high, 0, 1) + dot(proj, low, 0, 1)
        for q in range(BANDS):
            share_ref[q] = wide[q * SHARE : (q + 1) * SHARE].astype(BF16)


def tiles(count, source, target, grad, proj):
    return pl.pallas_call(
        tile_kernel,
        grid=(2,),
        in_specs=[
            pl.BlockSpec(memory_space=pltpu.SMEM),
            pl.BlockSpec((PIXELS, MID), lambda j: (0, 0)),
            pl.BlockSpec((1, PIXELS, MID), lambda j: (j, 0, 0)),
            pl.BlockSpec((1, 1, 1, PIXELS, 960), lambda j: (0, j, 0, 0, 0)),
            pl.BlockSpec((MID, 256), lambda j: (0, 0)),
        ],
        out_specs=[
            pl.BlockSpec((1, 1, 1, PIXELS, 960), lambda j: (0, j, 0, 0, 0)),
            pl.BlockSpec((BANDS, 1, MID, QUARTER), lambda j: (0, j, 0, 0)),
            pl.BlockSpec((BANDS, SHARE, PIXELS), lambda j: (0, 0, 0)),
        ],
        out_shape=[
            jax.ShapeDtypeStruct((1, 2, 1, PIXELS, 960), BF16),
            jax.ShapeDtypeStruct((BANDS, 2, MID, QUARTER), BF16),
            jax.ShapeDtypeStruct((BANDS, SHARE, PIXELS), BF16),
        ],
        scratch_shapes=[
            pltpu.VMEM((LOWER, PIXELS), BF16),
            pltpu.VMEM((PIXELS, 2 * MID), BF16),
            pltpu.VMEM((PIXELS, MID), F32),
        ],
    )(count, source, target, grad, proj)


def swap(parts):
    here = lax.axis_index("band")
    got = [lax.dynamic_index_in_dim(parts, here, 0, keepdims=False)]
    for d in range(1, BANDS):
        out = lax.dynamic_index_in_dim(parts, (here + d) % BANDS, 0, keepdims=False)
        got.append(lax.ppermute(out, "band", [(i, (i + d) % BANDS) for i in range(BANDS)]))
    return jnp.stack(got)[(here - jnp.arange(BANDS)) % BANDS]


def shards(frames, conv_weight, proj_weight, band_start, band_count, pyramid_grad):
    here = lax.axis_index("band")
    start = band_start[0]
    rim_row = shifted(frames[:, -1:], "rows", 1)
    convolved = lax.conv_general_dilated(
        jnp.concatenate([rim_row, frames], axis=1),
        conv_weight,
        (2, 2),
        ((0, 0), (1, 0)),
        dimension_numbers=("NHWC", "HWIO", "NHWC"),
        preferred_element_type=F32,
    )
    middle = jax.nn.relu(convolved).astype(BF16).reshape(2, PIXELS, MID)
    own = lax.dynamic_slice_in_dim(middle[1], here * QUARTER, QUARTER, 0)
    offsets = range(-BAND_REACH, BAND_REACH + 1)
    window = jnp.stack([own if o == 0 else shifted(own, "rows", -o) for o in offsets])
    places = start + BAND_REACH + jnp.arange(2)[None] * BANDS + jnp.arange(BANDS)[:, None]
    chosen = window[jnp.clip(places, 0, 2 * BAND_REACH)]
    target = jnp.swapaxes(swap(chosen), 0, 1).reshape(2, PIXELS, MID)
    pyramid, terms, share = tiles(band_count, middle[0], target, pyramid_grad, proj_weight)
    slots = jnp.swapaxes(swap(terms), 0, 1).reshape(8, MID, QUARTER)
    summed = jnp.zeros((MID, QUARTER), F32)
    for o in offsets:
        slot = o - start
        out = lax.dynamic_index_in_dim(slots, jnp.clip(slot, 0, 7), 0, keepdims=False)
        out = jnp.where((slot >= 0) & (slot < 8), out, jnp.zeros_like(out))
        summed = summed + (out if o == 0 else shifted(out, "rows", o)).astype(F32)
    high, low = halves(summed)
    wide = dot(proj_weight, high, 0, 0) + dot(proj_weight, low, 0, 0)
    target_share = jnp.swapaxes(swap(wide.reshape(BANDS, SHARE, QUARTER)), 1, 2)
    source_share = jnp.sum(swap(share).astype(F32), axis=0).T
    shape_out = (ROWS_DEV, PIXELS // ROWS_DEV, SHARE)
    return pyramid, source_share.reshape(shape_out), target_share.reshape(shape_out)


def solution(mesh):
    in_specs = (
        P(None, "rows", None, None),
        P(),
        P(),
        P("rows"),
        P("rows"),
        P("rows", None, "band", None, None),
    )
    out_specs = (
        P("rows", None, "band", None, None),
        P("rows", None, "band"),
        P("rows", None, "band"),
    )
    return jax.shard_map(shards, mesh=mesh, in_specs=in_specs, out_specs=out_specs, check_vma=False)
```

```python
import jax
import jax.numpy as jnp
from jax import lax
from jax.experimental import pallas as pl
from jax.experimental.pallas import tpu as pltpu
from jax.sharding import PartitionSpec as P

ROWS_DEV = 2
BAND_REACH = 4
PIXELS = 512
MID = 128
LOWER = 448
BANDS = 4
QUARTER = PIXELS // BANDS
SHARE = 64
SCALE = 1.0 / 16.0
F32 = jnp.float32
BF16 = jnp.bfloat16
MESH = pl.DeviceIdType.MESH
OFFSETS = (-4, 4, -3, 3, -2, 2, -1, 1)


def shifted(x, axis, by):
    size = lax.axis_size(axis)
    pairs = [(i, i + by) for i in range(size) if 0 <= i + by < size]
    return lax.ppermute(x, axis, pairs)


def halves(x):
    high = x.astype(BF16)
    return high, (x - high.astype(F32)).astype(BF16)


def dot(a, b, da=1, db=0):
    return lax.dot_general(a, b, (((da,), (db,)), ((), ())), preferred_element_type=F32)


def tile_kernel(count_ref, source_ref, target_ref, grad_ref, proj_ref, pyramid_ref, terms_ref, share_ref, pool, spread, pair, total):
    j = pl.program_id(0)
    source = source_ref[...]

    @pl.when(j == 0)
    def _():
        row = lax.broadcasted_iota(jnp.int32, (LOWER, PIXELS), 0)
        column = lax.broadcasted_iota(jnp.int32, (LOWER, PIXELS), 1)
        shift = jnp.where(row < 256, 1, jnp.where(row < 384, 2, 3))
        first = jnp.where(row < 256, 0, jnp.where(row < 384, 256, 384))
        weight = jnp.where(row < 256, 0.5, jnp.where(row < 384, 0.25, 0.125))
        pool[...] = jnp.where((column >> shift) == row - first, weight, 0.0).astype(BF16)
        square_high, square_low = halves(dot(proj_ref[...], proj_ref[...], 1, 1) * SCALE)
        high, low = halves(dot(source, square_high) + dot(source, square_low))
        pair[...] = jnp.concatenate([high, low], axis=1)
        row = lax.broadcasted_iota(jnp.int32, (PIXELS, LOWER), 0)
        column = lax.broadcasted_iota(jnp.int32, (PIXELS, LOWER), 1)
        shift = jnp.where(column < 256, 1, jnp.where(column < 384, 2, 3))
        first = jnp.where(column < 256, 0, jnp.where(column < 384, 256, 384))
        weight = jnp.where(column < 256, 0.5, jnp.where(column < 384, 0.25, 0.125))
        spread[...] = jnp.where((row >> shift) == column - first, weight, 0.0).astype(BF16)

    valid = j * BANDS + lax.axis_index("band") < count_ref[0]
    target = target_ref[0]
    grad = grad_ref[0, 0, 0]
    high, low = halves(dot(pool[...], target))
    base = dot(jnp.concatenate([target, target], axis=1), pair[...], 1, 1)
    rest = dot(jnp.concatenate([high, high], axis=1), pair[...], 1, 1) + dot(low, pair[:, :MID], 1, 1)
    pyramid_ref[0, 0, 0, :PIXELS] = jnp.where(valid, base, 0.0).astype(BF16)
    pyramid_ref[0, 0, 0, PIXELS:] = jnp.where(valid, rest, 0.0).astype(BF16)
    both = dot(jnp.concatenate([high, low], axis=1), grad[PIXELS:], 0, 0)
    part = jnp.where(valid, dot(target, grad[:PIXELS], 0, 0) + both[:MID] + both[MID:], 0.0)
    gathered = dot(grad, source)
    both = dot(spread[...], jnp.concatenate(halves(gathered[PIXELS:]), axis=1))
    term = (gathered[:PIXELS] + both[:, :MID] + both[:, MID:]) * SCALE
    term = jnp.where(valid, term, 0.0).astype(BF16)
    for q in range(BANDS):
        terms_ref[q, 0] = term[q * QUARTER : (q + 1) * QUARTER]

    @pl.when(j == 0)
    def _():
        total[...] = part

    @pl.when(j == 1)
    def _():
        high, low = halves((total[...] + part) * SCALE)
        proj = proj_ref[...]
        wide = dot(proj, high, 0, 0) + dot(proj, low, 0, 0)
        for q in range(BANDS):
            share_ref[q] = wide[q * SHARE : (q + 1) * SHARE].astype(BF16)


def tiles(count, source, target, grad, proj):
    return pl.pallas_call(
        tile_kernel,
        grid=(2,),
        in_specs=[
            pl.BlockSpec(memory_space=pltpu.SMEM),
            pl.BlockSpec((PIXELS, MID), lambda j: (0, 0)),
            pl.BlockSpec((1, PIXELS, MID), lambda j: (j, 0, 0)),
            pl.BlockSpec((1, 1, 1, 960, PIXELS), lambda j: (0, j, 0, 0, 0)),
            pl.BlockSpec((MID, 256), lambda j: (0, 0)),
        ],
        out_specs=[
            pl.BlockSpec((1, 1, 1, 960, PIXELS), lambda j: (0, j, 0, 0, 0)),
            pl.BlockSpec((BANDS, 1, QUARTER, MID), lambda j: (0, j, 0, 0)),
            pl.BlockSpec((BANDS, SHARE, PIXELS), lambda j: (0, 0, 0)),
        ],
        out_shape=[
            jax.ShapeDtypeStruct((1, 2, 1, 960, PIXELS), BF16),
            jax.ShapeDtypeStruct((BANDS, 2, QUARTER, MID), BF16),
            jax.ShapeDtypeStruct((BANDS, SHARE, PIXELS), BF16),
        ],
        scratch_shapes=[
            pltpu.VMEM((LOWER, PIXELS), BF16),
            pltpu.VMEM((PIXELS, LOWER), BF16),
            pltpu.VMEM((PIXELS, 2 * MID), BF16),
            pltpu.VMEM((MID, PIXELS), F32),
        ],
    )(count, source, target, grad, proj)


def band_peers():
    here = lax.axis_index("band")
    return here, [lax.rem(here + d, BANDS) for d in range(BANDS)]


def row_peer(offset):
    size = lax.axis_size("rows")
    return lax.rem(lax.axis_index("rows") + offset + size, size)


def in_frame(offset):
    block = lax.axis_index("rows") + offset
    return (block >= 0) & (block < lax.axis_size("rows"))


def meet(peers):
    barrier = pltpu.get_barrier_semaphore()
    for o in OFFSETS:
        pl.semaphore_signal(barrier, inc=1, device_id={"rows": row_peer(o)}, device_id_type=MESH)
    for d in range(1, BANDS):
        pl.semaphore_signal(barrier, inc=1, device_id={"band": peers[d]}, device_id_type=MESH)
    pl.semaphore_wait(barrier, len(OFFSETS) + BANDS - 1)


def send(source, target, sent, got, where):
    copy = pltpu.make_async_remote_copy(
        src_ref=source, dst_ref=target, send_sem=sent, recv_sem=got, device_id=where, device_id_type=MESH
    )
    copy.start()
    return copy


def fetch_kernel(start_ref, middle_ref, tiles_ref, window, chosen, row_sent, row_got, band_sent, band_got):
    here, peers = band_peers()
    meet(peers)
    own = middle_ref.at[1, pl.ds(pl.multiple_of(here * QUARTER, QUARTER), QUARTER)]
    copies = [
        send(own, window.at[o + BAND_REACH], row_sent.at[n], row_got.at[n], {"rows": row_peer(-o)})
        for n, o in enumerate(OFFSETS)
    ]
    window[BAND_REACH] = own[...]
    for copy in copies:
        copy.wait()
    start = start_ref[0]
    copies = []
    for d in (2, 1, 3, 0):
        for j in range(2):
            offset = start + j * BANDS + peers[d]
            place = jnp.minimum(offset + BAND_REACH, 2 * BAND_REACH)
            tile = jnp.where(in_frame(offset), window[place].astype(F32), 0.0).astype(BF16)
            if d == 0:
                tiles_ref[j, here] = tile
            else:
                chosen[d, j] = tile
        if d:
            copies.append(
                send(chosen.at[d], tiles_ref.at[:, here], band_sent.at[d], band_got.at[d], {"band": peers[d]})
            )
    for copy in copies:
        copy.wait()


def fetch(start, middle):
    return pl.pallas_call(
        fetch_kernel,
        in_specs=[pl.BlockSpec(memory_space=pltpu.SMEM), pl.BlockSpec(memory_space=pltpu.VMEM)],
        out_specs=pl.BlockSpec(memory_space=pltpu.VMEM),
        out_shape=jax.ShapeDtypeStruct((2, BANDS, QUARTER, MID), BF16),
        scratch_shapes=[
            pltpu.VMEM((2 * BAND_REACH + 1, QUARTER, MID), BF16),
            pltpu.VMEM((BANDS, 2, QUARTER, MID), BF16),
            pltpu.SemaphoreType.DMA((len(OFFSETS),)),
            pltpu.SemaphoreType.DMA((len(OFFSETS),)),
            pltpu.SemaphoreType.DMA((BANDS,)),
            pltpu.SemaphoreType.DMA((BANDS,)),
        ],
        compiler_params=pltpu.CompilerParams(collective_id=1, has_side_effects=True),
    )(start, middle)


def combine_kernel(
    start_ref, terms_ref, share_ref, proj_ref, source_ref, target_ref, slots, shares, stage, landed, wide, wides, row_sent, row_got, band_sent, band_got
):
    here, peers = band_peers()
    meet(peers)
    term_copies, share_copies, copies = [], [], []
    for d in (2, 1, 3):
        where = {"band": peers[d]}
        term_copies.append(send(terms_ref.at[peers[d]], slots.at[here], band_sent.at[0, d], band_got.at[0, d], where))
    for d in (2, 1, 3):
        where = {"band": peers[d]}
        share_copies.append(send(share_ref.at[peers[d]], shares.at[here], band_sent.at[1, d], band_got.at[1, d], where))
    slots[here] = terms_ref[here]
    shares[here] = share_ref[here]
    for copy in term_copies:
        copy.wait()
    start = start_ref[0]

    def picked(o):
        slot = o - start
        place = jnp.clip(slot, 0, 7)
        tile = slots[lax.rem(place, BANDS), lax.div(place, BANDS)].astype(F32)
        return jnp.where((slot >= 0) & (slot < 8), tile, 0.0)

    for n, o in enumerate(OFFSETS):
        stage[n] = picked(o).astype(BF16)
        copies.append(send(stage.at[n], landed.at[n], row_sent.at[n], row_got.at[n], {"rows": row_peer(o)}))
    summed = picked(0)
    for copy in share_copies:
        copy.wait()
    total = shares[0].astype(F32)
    for q in range(1, BANDS):
        total = total + shares[q].astype(F32)
    source_ref[0] = total[:, :256]
    source_ref[1] = total[:, 256:]
    for copy in copies:
        copy.wait()
    for n, o in enumerate(OFFSETS):
        summed = summed + jnp.where(in_frame(-o), landed[n].astype(F32), 0.0)
    high, low = halves(summed)
    proj = proj_ref[...]
    full = dot(proj, high, 0, 1) + dot(proj, low, 0, 1)
    for q in range(BANDS):
        wide[q] = full[q * SHARE : (q + 1) * SHARE]
    copies = [
        send(wide.at[peers[d]], wides.at[here], band_sent.at[2, d], band_got.at[2, d], {"band": peers[d]})
        for d in (2, 1, 3)
    ]
    wides[here] = wide[here]
    for copy in copies:
        copy.wait()
    for q in range(BANDS):
        target_ref[q // 2, :, (q % 2) * QUARTER : (q % 2 + 1) * QUARTER] = wides[q]


def combine(start, terms, share, proj):
    vmem = pl.BlockSpec(memory_space=pltpu.VMEM)
    return pl.pallas_call(
        combine_kernel,
        in_specs=[pl.BlockSpec(memory_space=pltpu.SMEM), vmem, vmem, vmem],
        out_specs=[vmem, vmem],
        out_shape=[jax.ShapeDtypeStruct((ROWS_DEV, SHARE, PIXELS // ROWS_DEV), F32)] * 2,
        scratch_shapes=[
            pltpu.VMEM((BANDS, 2, QUARTER, MID), BF16),
            pltpu.VMEM((BANDS, SHARE, PIXELS), BF16),
            pltpu.VMEM((len(OFFSETS), QUARTER, MID), BF16),
            pltpu.VMEM((len(OFFSETS), QUARTER, MID), BF16),
            pltpu.VMEM((BANDS, SHARE, QUARTER), F32),
            pltpu.VMEM((BANDS, SHARE, QUARTER), F32),
            pltpu.SemaphoreType.DMA((len(OFFSETS),)),
            pltpu.SemaphoreType.DMA((len(OFFSETS),)),
            pltpu.SemaphoreType.DMA((3, BANDS)),
            pltpu.SemaphoreType.DMA((3, BANDS)),
        ],
        compiler_params=pltpu.CompilerParams(collective_id=2, has_side_effects=True),
    )(start, terms, share, proj)


def shards(frames, conv_weight, proj_weight, band_start, band_count, pyramid_grad):
    rim_row = shifted(frames[:, -1:], "rows", 1)
    convolved = lax.conv_general_dilated(
        jnp.concatenate([rim_row, frames], axis=1),
        conv_weight,
        (2, 2),
        ((0, 0), (1, 0)),
        dimension_numbers=("NHWC", "HWIO", "NHWC"),
        preferred_element_type=F32,
    )
    middle = jax.nn.relu(convolved).astype(BF16).reshape(2, PIXELS, MID)
    target = fetch(band_start, middle).reshape(2, PIXELS, MID)
    pyramid, terms, share = tiles(band_count, middle[0], target, jnp.swapaxes(pyramid_grad, 3, 4), proj_weight)
    source_share, target_share = combine(band_start, terms, share, proj_weight)
    return jnp.swapaxes(pyramid, 3, 4), jnp.swapaxes(source_share, 1, 2), jnp.swapaxes(target_share, 1, 2)


def solution(mesh):
    in_specs = (
        P(None, "rows", None, None),
        P(),
        P(),
        P("rows"),
        P("rows"),
        P("rows", None, "band", None, None),
    )
    out_specs = (
        P("rows", None, "band", None, None),
        P("rows", None, "band"),
        P("rows", None, "band"),
    )
    return jax.shard_map(shards, mesh=mesh, in_specs=in_specs, out_specs=out_specs, check_vma=False)
```

```python
import jax
import jax.numpy as jnp
from jax import lax
from jax.experimental import pallas as pl
from jax.experimental.pallas import tpu as pltpu
from jax.sharding import PartitionSpec as P

ROWS_DEV = 2
BAND_REACH = 4
PIXELS = 512
MID = 128
LOWER = 448
BANDS = 4
QUARTER = PIXELS // BANDS
SHARE = 64
SCALE = 1.0 / 16.0
F32 = jnp.float32
BF16 = jnp.bfloat16
MESH = pl.DeviceIdType.MESH
OFFSETS = (-4, 4, -3, 3, -2, 2, -1, 1)


def halves(x):
    high = x.astype(BF16)
    return high, (x - high.astype(F32)).astype(BF16)


def dot(a, b, da=1, db=0):
    return lax.dot_general(a, b, (((da,), (db,)), ((), ())), preferred_element_type=F32)


def tile_kernel(count_ref, source_ref, target_ref, grad_ref, proj_ref, pyramid_ref, terms_ref, share_ref, pool, spread, pair, total):
    j = pl.program_id(0)
    source = source_ref[...]

    @pl.when(j == 0)
    def _():
        row = lax.broadcasted_iota(jnp.int32, (LOWER, PIXELS), 0)
        column = lax.broadcasted_iota(jnp.int32, (LOWER, PIXELS), 1)
        shift = jnp.where(row < 256, 1, jnp.where(row < 384, 2, 3))
        first = jnp.where(row < 256, 0, jnp.where(row < 384, 256, 384))
        weight = jnp.where(row < 256, 0.5, jnp.where(row < 384, 0.25, 0.125))
        pool[...] = jnp.where((column >> shift) == row - first, weight, 0.0).astype(BF16)
        square_high, square_low = halves(dot(proj_ref[...], proj_ref[...], 1, 1) * SCALE)
        high, low = halves(dot(source, square_high) + dot(source, square_low))
        pair[...] = jnp.concatenate([high, low], axis=1)
        row = lax.broadcasted_iota(jnp.int32, (PIXELS, LOWER), 0)
        column = lax.broadcasted_iota(jnp.int32, (PIXELS, LOWER), 1)
        shift = jnp.where(column < 256, 1, jnp.where(column < 384, 2, 3))
        first = jnp.where(column < 256, 0, jnp.where(column < 384, 256, 384))
        weight = jnp.where(column < 256, 0.5, jnp.where(column < 384, 0.25, 0.125))
        spread[...] = jnp.where((row >> shift) == column - first, weight, 0.0).astype(BF16)

    valid = j * BANDS + lax.axis_index("band") < count_ref[0]
    target = target_ref[0]
    grad = grad_ref[0, 0, 0]
    high, low = halves(dot(pool[...], target))
    base = dot(jnp.concatenate([target, target], axis=1), pair[...], 1, 1)
    rest = dot(jnp.concatenate([high, high], axis=1), pair[...], 1, 1) + dot(low, pair[:, :MID], 1, 1)
    pyramid_ref[0, 0, 0, :PIXELS] = jnp.where(valid, base, 0.0).astype(BF16)
    pyramid_ref[0, 0, 0, PIXELS:] = jnp.where(valid, rest, 0.0).astype(BF16)
    both = dot(jnp.concatenate([high, low], axis=1), grad[PIXELS:], 0, 0)
    part = jnp.where(valid, dot(target, grad[:PIXELS], 0, 0) + both[:MID] + both[MID:], 0.0)
    gathered = dot(grad, source)
    both = dot(spread[...], jnp.concatenate(halves(gathered[PIXELS:]), axis=1))
    term = (gathered[:PIXELS] + both[:, :MID] + both[:, MID:]) * SCALE
    term = jnp.where(valid, term, 0.0).astype(BF16)
    for q in range(BANDS):
        terms_ref[q, 0] = term[q * QUARTER : (q + 1) * QUARTER]

    @pl.when(j == 0)
    def _():
        total[...] = part

    @pl.when(j == 1)
    def _():
        high, low = halves((total[...] + part) * SCALE)
        proj = proj_ref[...]
        wide = dot(proj, high, 0, 0) + dot(proj, low, 0, 0)
        for q in range(BANDS):
            share_ref[q] = wide[q * SHARE : (q + 1) * SHARE].astype(BF16)


def tiles(count, source, target, grad, proj):
    return pl.pallas_call(
        tile_kernel,
        grid=(2,),
        in_specs=[
            pl.BlockSpec(memory_space=pltpu.SMEM),
            pl.BlockSpec((PIXELS, MID), lambda j: (0, 0)),
            pl.BlockSpec((1, PIXELS, MID), lambda j: (j, 0, 0)),
            pl.BlockSpec((1, 1, 1, 960, PIXELS), lambda j: (0, j, 0, 0, 0)),
            pl.BlockSpec((MID, 256), lambda j: (0, 0)),
        ],
        out_specs=[
            pl.BlockSpec((1, 1, 1, 960, PIXELS), lambda j: (0, j, 0, 0, 0)),
            pl.BlockSpec((BANDS, 1, QUARTER, MID), lambda j: (0, j, 0, 0)),
            pl.BlockSpec((BANDS, SHARE, PIXELS), lambda j: (0, 0, 0)),
        ],
        out_shape=[
            jax.ShapeDtypeStruct((1, 2, 1, 960, PIXELS), BF16),
            jax.ShapeDtypeStruct((BANDS, 2, QUARTER, MID), BF16),
            jax.ShapeDtypeStruct((BANDS, SHARE, PIXELS), BF16),
        ],
        scratch_shapes=[
            pltpu.VMEM((LOWER, PIXELS), BF16),
            pltpu.VMEM((PIXELS, LOWER), BF16),
            pltpu.VMEM((PIXELS, 2 * MID), BF16),
            pltpu.VMEM((MID, PIXELS), F32),
        ],
    )(count, source, target, grad, proj)


def band_peers():
    here = lax.axis_index("band")
    return here, [lax.rem(here + d, BANDS) for d in range(BANDS)]


def row_peer(offset):
    size = lax.axis_size("rows")
    return lax.rem(lax.axis_index("rows") + offset + size, size)


def in_frame(offset):
    block = lax.axis_index("rows") + offset
    return (block >= 0) & (block < lax.axis_size("rows"))


def meet(peers):
    barrier = pltpu.get_barrier_semaphore()
    for o in OFFSETS:
        pl.semaphore_signal(barrier, inc=1, device_id={"rows": row_peer(o)}, device_id_type=MESH)
    for d in range(1, BANDS):
        pl.semaphore_signal(barrier, inc=1, device_id={"band": peers[d]}, device_id_type=MESH)
    return barrier


def send(source, target, sent, got, where):
    copy = pltpu.make_async_remote_copy(
        src_ref=source, dst_ref=target, send_sem=sent, recv_sem=got, device_id=where, device_id_type=MESH
    )
    copy.start()
    return copy


def fetch_kernel(
    start_ref, frames_ref, conv_ref, tiles_ref, source_ref, rim, middle, taps, window, chosen, rim_sent, rim_got, row_sent, row_got, band_sent, band_got
):
    here, peers = band_peers()
    barrier = meet(peers)
    weight = jnp.concatenate([conv_ref[:, dx].reshape(3 * 96, MID) for dx in range(3)], axis=1)

    def convolve(stack, out, r):
        full = dot(stack, weight, 0, 0)
        for dx in range(3):
            taps[dx, 8 : 8 + PIXELS] = full[:, dx * MID : (dx + 1) * MID]
        total = taps[0, pl.ds(7, 256, stride=2)] + taps[1, pl.ds(8, 256, stride=2)] + taps[2, pl.ds(9, 256, stride=2)]
        out[r * 256 : (r + 1) * 256] = jnp.maximum(total, 0.0).astype(BF16)

    def first_row(f):
        above = jnp.where(in_frame(-1), rim[f].astype(F32), 0.0).astype(BF16)
        return jnp.concatenate([above, frames_ref[f, 0], frames_ref[f, 1]], axis=0)

    taps[0, :8] = jnp.zeros((8, MID), F32)
    convolve(frames_ref[1, 1:4].reshape(3 * 96, PIXELS), middle, 1)
    pl.semaphore_wait(barrier, len(OFFSETS) + BANDS - 1)
    rims = [
        send(frames_ref.at[f, 3], rim.at[f], rim_sent.at[f], rim_got.at[f], {"rows": row_peer(1)}) for f in (1, 0)
    ]
    convolve(frames_ref[0, 1:4].reshape(3 * 96, PIXELS), source_ref, 1)
    rims[0].wait()
    convolve(first_row(1), middle, 0)
    own = middle.at[pl.ds(pl.multiple_of(here * QUARTER, QUARTER), QUARTER)]
    copies = [
        send(own, window.at[o + BAND_REACH], row_sent.at[n], row_got.at[n], {"rows": row_peer(-o)})
        for n, o in enumerate(OFFSETS)
    ]
    rims[1].wait()
    convolve(first_row(0), source_ref, 0)
    window[BAND_REACH] = own[...]
    for copy in copies:
        copy.wait()
    start = start_ref[0]
    copies = []
    for d in (2, 1, 3, 0):
        for j in range(2):
            offset = start + j * BANDS + peers[d]
            place = jnp.minimum(offset + BAND_REACH, 2 * BAND_REACH)
            tile = jnp.where(in_frame(offset), window[place].astype(F32), 0.0).astype(BF16)
            if d == 0:
                tiles_ref[j, here] = tile
            else:
                chosen[d, j] = tile
        if d:
            copies.append(
                send(chosen.at[d], tiles_ref.at[:, here], band_sent.at[d], band_got.at[d], {"band": peers[d]})
            )
    for copy in copies:
        copy.wait()


def fetch(start, frames, conv):
    vmem = pl.BlockSpec(memory_space=pltpu.VMEM)
    return pl.pallas_call(
        fetch_kernel,
        in_specs=[pl.BlockSpec(memory_space=pltpu.SMEM), vmem, vmem],
        out_specs=[vmem, vmem],
        out_shape=[
            jax.ShapeDtypeStruct((2, BANDS, QUARTER, MID), BF16),
            jax.ShapeDtypeStruct((PIXELS, MID), BF16),
        ],
        scratch_shapes=[
            pltpu.VMEM((2, 96, PIXELS), BF16),
            pltpu.VMEM((PIXELS, MID), BF16),
            pltpu.VMEM((3, PIXELS + 16, MID), F32),
            pltpu.VMEM((2 * BAND_REACH + 1, QUARTER, MID), BF16),
            pltpu.VMEM((BANDS, 2, QUARTER, MID), BF16),
            pltpu.SemaphoreType.DMA((2,)),
            pltpu.SemaphoreType.DMA((2,)),
            pltpu.SemaphoreType.DMA((len(OFFSETS),)),
            pltpu.SemaphoreType.DMA((len(OFFSETS),)),
            pltpu.SemaphoreType.DMA((BANDS,)),
            pltpu.SemaphoreType.DMA((BANDS,)),
        ],
        compiler_params=pltpu.CompilerParams(collective_id=1, has_side_effects=True),
    )(start, frames, conv)


def combine_kernel(
    start_ref, terms_ref, share_ref, proj_ref, source_ref, wides, slots, shares, stage, landed, wide, row_sent, row_got, band_sent, band_got
):
    here, peers = band_peers()
    pl.semaphore_wait(meet(peers), len(OFFSETS) + BANDS - 1)
    term_copies, share_copies, copies = [], [], []
    for d in (2, 1, 3):
        where = {"band": peers[d]}
        term_copies.append(send(terms_ref.at[peers[d]], slots.at[here], band_sent.at[0, d], band_got.at[0, d], where))
    for d in (2, 1, 3):
        where = {"band": peers[d]}
        share_copies.append(send(share_ref.at[peers[d]], shares.at[here], band_sent.at[1, d], band_got.at[1, d], where))
    slots[here] = terms_ref[here]
    shares[here] = share_ref[here]
    for copy in term_copies:
        copy.wait()
    start = start_ref[0]

    def picked(o):
        slot = o - start
        place = jnp.clip(slot, 0, 7)
        tile = slots[lax.rem(place, BANDS), lax.div(place, BANDS)].astype(F32)
        return jnp.where((slot >= 0) & (slot < 8), tile, 0.0)

    for n, o in enumerate(OFFSETS):
        stage[n] = picked(o).astype(BF16)
        copies.append(send(stage.at[n], landed.at[n], row_sent.at[n], row_got.at[n], {"rows": row_peer(o)}))
    summed = picked(0)
    for copy in share_copies:
        copy.wait()
    total = shares[0].astype(F32)
    for q in range(1, BANDS):
        total = total + shares[q].astype(F32)
    source_ref[0] = total[:, :256]
    source_ref[1] = total[:, 256:]
    for copy in copies:
        copy.wait()
    for n, o in enumerate(OFFSETS):
        summed = summed + jnp.where(in_frame(-o), landed[n].astype(F32), 0.0)
    high, low = halves(summed)
    proj = proj_ref[...]
    full = dot(proj, high, 0, 1) + dot(proj, low, 0, 1)
    for q in range(BANDS):
        wide[q] = full[q * SHARE : (q + 1) * SHARE]
    copies = [
        send(wide.at[peers[d]], wides.at[here], band_sent.at[2, d], band_got.at[2, d], {"band": peers[d]})
        for d in (2, 1, 3)
    ]
    wides[here] = wide[here]
    for copy in copies:
        copy.wait()


def combine(start, terms, share, proj):
    vmem = pl.BlockSpec(memory_space=pltpu.VMEM)
    return pl.pallas_call(
        combine_kernel,
        in_specs=[pl.BlockSpec(memory_space=pltpu.SMEM), vmem, vmem, vmem],
        out_specs=[vmem, vmem],
        out_shape=[
            jax.ShapeDtypeStruct((ROWS_DEV, SHARE, PIXELS // ROWS_DEV), F32),
            jax.ShapeDtypeStruct((BANDS, SHARE, QUARTER), F32),
        ],
        scratch_shapes=[
            pltpu.VMEM((BANDS, 2, QUARTER, MID), BF16),
            pltpu.VMEM((BANDS, SHARE, PIXELS), BF16),
            pltpu.VMEM((len(OFFSETS), QUARTER, MID), BF16),
            pltpu.VMEM((len(OFFSETS), QUARTER, MID), BF16),
            pltpu.VMEM((BANDS, SHARE, QUARTER), F32),
            pltpu.SemaphoreType.DMA((len(OFFSETS),)),
            pltpu.SemaphoreType.DMA((len(OFFSETS),)),
            pltpu.SemaphoreType.DMA((3, BANDS)),
            pltpu.SemaphoreType.DMA((3, BANDS)),
        ],
        compiler_params=pltpu.CompilerParams(collective_id=2, has_side_effects=True),
    )(start, terms, share, proj)


def finish_kernel(summed_ref, wides_ref, source_ref, target_ref):
    source_ref[...] = summed_ref[...]
    for q in range(BANDS):
        target_ref[q // 2, :, (q % 2) * QUARTER : (q % 2 + 1) * QUARTER] = wides_ref[q]


def finish(summed, wides):
    vmem = pl.BlockSpec(memory_space=pltpu.VMEM)
    return pl.pallas_call(
        finish_kernel,
        in_specs=[vmem, vmem],
        out_specs=[vmem, vmem],
        out_shape=[jax.ShapeDtypeStruct((ROWS_DEV, SHARE, PIXELS // ROWS_DEV), F32)] * 2,
    )(summed, wides)


def shards(frames, conv_weight, proj_weight, band_start, band_count, pyramid_grad):
    target, source = fetch(band_start, jnp.swapaxes(frames, 2, 3), conv_weight)
    target = target.reshape(2, PIXELS, MID)
    pyramid, terms, share = tiles(band_count, source, target, jnp.swapaxes(pyramid_grad, 3, 4), proj_weight)
    source_share, target_share = finish(*combine(band_start, terms, share, proj_weight))
    return jnp.swapaxes(pyramid, 3, 4), jnp.swapaxes(source_share, 1, 2), jnp.swapaxes(target_share, 1, 2)


def solution(mesh):
    in_specs = (
        P(None, "rows", None, None),
        P(),
        P(),
        P("rows"),
        P("rows"),
        P("rows", None, "band", None, None),
    )
    out_specs = (
        P("rows", None, "band", None, None),
        P("rows", None, "band"),
        P("rows", None, "band"),
    )
    return jax.shard_map(shards, mesh=mesh, in_specs=in_specs, out_specs=out_specs, check_vma=False)
```

```python
import jax
import jax.numpy as jnp
from jax import lax
from jax.experimental import pallas as pl
from jax.experimental.pallas import tpu as pltpu
from jax.sharding import PartitionSpec as P

ROWS_DEV = 2
BAND_REACH = 4
PIXELS = 512
MID = 128
LOWER = 448
BANDS = 4
QUARTER = PIXELS // BANDS
SHARE = 64
SCALE = 1.0 / 16.0
F32 = jnp.float32
BF16 = jnp.bfloat16
MESH = pl.DeviceIdType.MESH
OFFSETS = (-4, 4, -3, 3, -2, 2, -1, 1)


def halves(x):
    high = x.astype(BF16)
    return high, (x - high.astype(F32)).astype(BF16)


def dot(a, b, da=1, db=0):
    return lax.dot_general(a, b, (((da,), (db,)), ((), ())), preferred_element_type=F32)


def pooling(shape, pixel_axis):
    pixel = lax.broadcasted_iota(jnp.int32, shape, pixel_axis)
    group = lax.broadcasted_iota(jnp.int32, shape, 1 - pixel_axis)
    shift = jnp.where(group < 256, 1, jnp.where(group < 384, 2, 3))
    first = jnp.where(group < 256, 0, jnp.where(group < 384, 256, 384))
    weight = jnp.where(group < 256, 0.5, jnp.where(group < 384, 0.25, 0.125))
    return jnp.where((pixel >> shift) == group - first, weight, 0.0).astype(BF16)


def tile_kernel(count_ref, source_ref, target_ref, proj_ref, summed_ref, wides_ref, pyramid_ref, sg_ref, tg_ref, pool, pair):
    j = pl.program_id(0)

    @pl.when(j == 0)
    def _():
        source = source_ref[...]
        pool[...] = pooling((LOWER, PIXELS), 1)
        square_high, square_low = halves(dot(proj_ref[...], proj_ref[...], 1, 1) * SCALE)
        high, low = halves(dot(source, square_high) + dot(source, square_low))
        pair[...] = jnp.concatenate([high, low], axis=1)
        sg_ref[...] = summed_ref[...]
        for q in range(BANDS):
            tg_ref[q // 2, :, (q % 2) * QUARTER : (q % 2 + 1) * QUARTER] = wides_ref[q]

    valid = j * BANDS + lax.axis_index("band") < count_ref[0]
    target = target_ref[0]
    high, low = halves(dot(pool[...], target))
    base = dot(jnp.concatenate([target, target], axis=1), pair[...], 1, 1)
    rest = dot(jnp.concatenate([high, high], axis=1), pair[...], 1, 1) + dot(low, pair[:, :MID], 1, 1)
    pyramid_ref[0, 0, 0, :PIXELS] = jnp.where(valid, base, 0.0).astype(BF16)
    pyramid_ref[0, 0, 0, PIXELS:] = jnp.where(valid, rest, 0.0).astype(BF16)


def tiles(count, source, target, proj, summed, wides):
    share = (ROWS_DEV, SHARE, PIXELS // ROWS_DEV)
    return pl.pallas_call(
        tile_kernel,
        grid=(2,),
        in_specs=[
            pl.BlockSpec(memory_space=pltpu.SMEM),
            pl.BlockSpec((PIXELS, MID), lambda j: (0, 0)),
            pl.BlockSpec((1, PIXELS, MID), lambda j: (j, 0, 0)),
            pl.BlockSpec((MID, 256), lambda j: (0, 0)),
            pl.BlockSpec(share, lambda j: (0, 0, 0)),
            pl.BlockSpec((BANDS, SHARE, QUARTER), lambda j: (0, 0, 0)),
        ],
        out_specs=[
            pl.BlockSpec((1, 1, 1, 960, PIXELS), lambda j: (0, j, 0, 0, 0)),
            pl.BlockSpec(share, lambda j: (0, 0, 0)),
            pl.BlockSpec(share, lambda j: (0, 0, 0)),
        ],
        out_shape=[
            jax.ShapeDtypeStruct((1, 2, 1, 960, PIXELS), BF16),
            jax.ShapeDtypeStruct(share, F32),
            jax.ShapeDtypeStruct(share, F32),
        ],
        scratch_shapes=[pltpu.VMEM((LOWER, PIXELS), BF16), pltpu.VMEM((PIXELS, 2 * MID), BF16)],
    )(count, source, target, proj, summed, wides)


def band_peers():
    here = lax.axis_index("band")
    return here, [lax.rem(here + d, BANDS) for d in range(BANDS)]


def row_peer(offset):
    size = lax.axis_size("rows")
    return lax.rem(lax.axis_index("rows") + offset + size, size)


def in_frame(offset):
    block = lax.axis_index("rows") + offset
    return (block >= 0) & (block < lax.axis_size("rows"))


def meet(peers):
    barrier = pltpu.get_barrier_semaphore()
    for o in OFFSETS:
        pl.semaphore_signal(barrier, inc=1, device_id={"rows": row_peer(o)}, device_id_type=MESH)
    for d in range(1, BANDS):
        pl.semaphore_signal(barrier, inc=1, device_id={"band": peers[d]}, device_id_type=MESH)
    return barrier


def send(source, target, sent, got, where):
    copy = pltpu.make_async_remote_copy(
        src_ref=source, dst_ref=target, send_sem=sent, recv_sem=got, device_id=where, device_id_type=MESH
    )
    copy.start()
    return copy


def fetch_kernel(
    start_ref, count_ref, frames_ref, conv_ref, proj_ref, grad_ref, tiles_ref, source_ref, summed_ref, wides,
    rim, middle, taps, window, chosen, spread, pool, terms, slots, share, shares, stage, landed, wide,
    rim_sent, rim_got, row_sent, row_got, band_sent, band_got
):
    here, peers = band_peers()
    barrier = meet(peers)
    weight = jnp.concatenate([conv_ref[:, dx].reshape(3 * 96, MID) for dx in range(3)], axis=1)

    def convolve(stack, out, r):
        full = dot(stack, weight, 0, 0)
        for dx in range(3):
            taps[dx, 8 : 8 + PIXELS] = full[:, dx * MID : (dx + 1) * MID]
        total = taps[0, pl.ds(7, 256, stride=2)] + taps[1, pl.ds(8, 256, stride=2)] + taps[2, pl.ds(9, 256, stride=2)]
        out[r * 256 : (r + 1) * 256] = jnp.maximum(total, 0.0).astype(BF16)

    def first_row(f):
        above = jnp.where(in_frame(-1), rim[f].astype(F32), 0.0).astype(BF16)
        return jnp.concatenate([above, frames_ref[f, 0], frames_ref[f, 1]], axis=0)

    taps[0, :8] = jnp.zeros((8, MID), F32)
    convolve(frames_ref[1, 1:4].reshape(3 * 96, PIXELS), middle, 1)
    pl.semaphore_wait(barrier, len(OFFSETS) + BANDS - 1)
    rims = [
        send(frames_ref.at[f, 3], rim.at[f], rim_sent.at[f], rim_got.at[f], {"rows": row_peer(1)}) for f in (1, 0)
    ]
    convolve(frames_ref[0, 1:4].reshape(3 * 96, PIXELS), source_ref, 1)
    spread[...] = pooling((PIXELS, LOWER), 0)
    pool[...] = pooling((LOWER, PIXELS), 1)
    rims[0].wait()
    convolve(first_row(1), middle, 0)
    own = middle.at[pl.ds(pl.multiple_of(here * QUARTER, QUARTER), QUARTER)]
    copies = [
        send(own, window.at[o + BAND_REACH], row_sent.at[0, n], row_got.at[0, n], {"rows": row_peer(-o)})
        for n, o in enumerate(OFFSETS)
    ]
    rims[1].wait()
    convolve(first_row(0), source_ref, 0)
    window[BAND_REACH] = own[...]
    source = source_ref[...]
    for j in range(2):
        gathered = dot(grad_ref[0, j, 0], source)
        both = dot(spread[...], jnp.concatenate(halves(gathered[PIXELS:]), axis=1))
        term = (gathered[:PIXELS] + both[:, :MID] + both[:, MID:]) * SCALE
        term = jnp.where(j * BANDS + here < count_ref[0], term, 0.0).astype(BF16)
        for q in range(BANDS):
            terms[q, j] = term[q * QUARTER : (q + 1) * QUARTER]

    def across(kind, outgoing, incoming):
        return [
            send(outgoing.at[peers[d]], incoming.at[here], band_sent.at[kind, d], band_got.at[kind, d], {"band": peers[d]})
            for d in (2, 1, 3)
        ]

    term_copies = across(0, terms, slots)
    slots[here] = terms[here]
    for copy in copies:
        copy.wait()
    start = start_ref[0]
    tile_copies = []
    for d in (2, 1, 3, 0):
        for j in range(2):
            offset = start + j * BANDS + peers[d]
            place = jnp.minimum(offset + BAND_REACH, 2 * BAND_REACH)
            tile = jnp.where(in_frame(offset), window[place].astype(F32), 0.0).astype(BF16)
            if d == 0:
                tiles_ref[j, here] = tile
            else:
                chosen[d, j] = tile
        if d:
            tile_copies.append(
                send(chosen.at[d], tiles_ref.at[:, here], band_sent.at[1, d], band_got.at[1, d], {"band": peers[d]})
            )
    for copy in term_copies:
        copy.wait()

    def picked(o):
        slot = o - start
        place = jnp.clip(slot, 0, 7)
        tile = slots[lax.rem(place, BANDS), lax.div(place, BANDS)].astype(F32)
        return jnp.where((slot >= 0) & (slot < 8), tile, 0.0)

    copies = []
    for n, o in enumerate(OFFSETS):
        stage[n] = picked(o).astype(BF16)
        copies.append(send(stage.at[n], landed.at[n], row_sent.at[1, n], row_got.at[1, n], {"rows": row_peer(o)}))
    summed = picked(0)
    for copy in tile_copies:
        copy.wait()
    total = jnp.zeros((MID, PIXELS), F32)
    for j in range(2):
        target = tiles_ref[j].reshape(PIXELS, MID)
        lower = jnp.concatenate(halves(dot(pool[...], target)), axis=1)
        both = dot(lower, grad_ref[0, j, 0, PIXELS:], 0, 0)
        part = dot(target, grad_ref[0, j, 0, :PIXELS], 0, 0) + both[:MID] + both[MID:]
        total = total + jnp.where(j * BANDS + here < count_ref[0], part, 0.0)
    high, low = halves(total * SCALE)
    proj = proj_ref[...]
    full = dot(proj, high, 0, 0) + dot(proj, low, 0, 0)
    for q in range(BANDS):
        share[q] = full[q * SHARE : (q + 1) * SHARE].astype(BF16)
    share_copies = across(2, share, shares)
    shares[here] = share[here]
    for copy in copies:
        copy.wait()
    for n, o in enumerate(OFFSETS):
        summed = summed + jnp.where(in_frame(-o), landed[n].astype(F32), 0.0)
    high, low = halves(summed)
    full = dot(proj, high, 0, 1) + dot(proj, low, 0, 1)
    for q in range(BANDS):
        wide[q] = full[q * SHARE : (q + 1) * SHARE]
    wide_copies = across(3, wide, wides)
    wides[here] = wide[here]
    for copy in share_copies:
        copy.wait()
    total = shares[0].astype(F32)
    for q in range(1, BANDS):
        total = total + shares[q].astype(F32)
    summed_ref[0] = total[:, :256]
    summed_ref[1] = total[:, 256:]
    for copy in wide_copies:
        copy.wait()


def fetch(start, count, frames, conv, proj, grad):
    vmem = pl.BlockSpec(memory_space=pltpu.VMEM)
    smem = pl.BlockSpec(memory_space=pltpu.SMEM)
    return pl.pallas_call(
        fetch_kernel,
        in_specs=[smem, smem, vmem, vmem, vmem, vmem],
        out_specs=[vmem] * 4,
        out_shape=[
            jax.ShapeDtypeStruct((2, BANDS, QUARTER, MID), BF16),
            jax.ShapeDtypeStruct((PIXELS, MID), BF16),
            jax.ShapeDtypeStruct((ROWS_DEV, SHARE, PIXELS // ROWS_DEV), F32),
            jax.ShapeDtypeStruct((BANDS, SHARE, QUARTER), F32),
        ],
        scratch_shapes=[
            pltpu.VMEM((2, 96, PIXELS), BF16),
            pltpu.VMEM((PIXELS, MID), BF16),
            pltpu.VMEM((3, PIXELS + 16, MID), F32),
            pltpu.VMEM((2 * BAND_REACH + 1, QUARTER, MID), BF16),
            pltpu.VMEM((BANDS, 2, QUARTER, MID), BF16),
            pltpu.VMEM((PIXELS, LOWER), BF16),
            pltpu.VMEM((LOWER, PIXELS), BF16),
            pltpu.VMEM((BANDS, 2, QUARTER, MID), BF16),
            pltpu.VMEM((BANDS, 2, QUARTER, MID), BF16),
            pltpu.VMEM((BANDS, SHARE, PIXELS), BF16),
            pltpu.VMEM((BANDS, SHARE, PIXELS), BF16),
            pltpu.VMEM((len(OFFSETS), QUARTER, MID), BF16),
            pltpu.VMEM((len(OFFSETS), QUARTER, MID), BF16),
            pltpu.VMEM((BANDS, SHARE, QUARTER), F32),
            pltpu.SemaphoreType.DMA((2,)),
            pltpu.SemaphoreType.DMA((2,)),
            pltpu.SemaphoreType.DMA((2, len(OFFSETS))),
            pltpu.SemaphoreType.DMA((2, len(OFFSETS))),
            pltpu.SemaphoreType.DMA((4, BANDS)),
            pltpu.SemaphoreType.DMA((4, BANDS)),
        ],
        compiler_params=pltpu.CompilerParams(collective_id=1, has_side_effects=True),
    )(start, count, frames, conv, proj, grad)


def shards(frames, conv_weight, proj_weight, band_start, band_count, pyramid_grad):
    target, source, summed, wides = fetch(
        band_start, band_count, jnp.swapaxes(frames, 2, 3), conv_weight, proj_weight, jnp.swapaxes(pyramid_grad, 3, 4)
    )
    pyramid, source_share, target_share = tiles(
        band_count, source, target.reshape(2, PIXELS, MID), proj_weight, summed, wides
    )
    return jnp.swapaxes(pyramid, 3, 4), jnp.swapaxes(source_share, 1, 2), jnp.swapaxes(target_share, 1, 2)


def solution(mesh):
    in_specs = (
        P(None, "rows", None, None),
        P(),
        P(),
        P("rows"),
        P("rows"),
        P("rows", None, "band", None, None),
    )
    out_specs = (
        P("rows", None, "band", None, None),
        P("rows", None, "band"),
        P("rows", None, "band"),
    )
    return jax.shard_map(shards, mesh=mesh, in_specs=in_specs, out_specs=out_specs, check_vma=False)
```
